32 devices in a mesh: dp: 8 (over z, x), adapter: 2 (over y), mp: 2 (over core).
Axes of the slice: x: 2, y: 2, z: 4, core: 2. Of those that a mesh axis runs over, the one named last changes fastest.
Arguments:
- tokens: bfloat16 [3456, 8192], P(('dp', 'adapter')), may hold values from -6 to 6
- base_weight: bfloat16 [8192, 512], P('dp', 'mp'), may hold values from -0.0625 to 0.0625
- adapter_a: bfloat16 [2, 64, 8192], P('adapter'), may hold values from -0.0625 to 0.0625
- adapter_b: bfloat16 [2, 64, 512], P('adapter', None, 'mp'), may hold values from -0.75 to 0.75
- cotangent: bfloat16 [3456, 512], P(('dp', 'adapter'), 'mp'), may hold values from -0.15625 to 0.15625
- adapter_ids: int32 [3456], P(('dp', 'adapter')), may hold values from 0 to 1, as said below
Outputs:
- projected: bfloat16 [3456, 512], P(('dp', 'adapter'), 'mp')
- grad_a: float32 [2, 64, 8192], P('adapter', 'dp', 'mp')
- up_gradient: float32 [2, 64, 512], P('adapter', 'dp', 'mp')
The draws below stay inside these ranges and needn't reach their ends.
Inputs may be any that keep to these rules, and one draw needn't show every extreme that they name: Among the 216 tokens of one device (aligned blocks of adapter_ids), no adapter occurs more than 144 times, some adapter occurs exactly 144 times, and every adapter occurs at least once.
All inputs are finite; a program needn't handle non-finite values.
Results may differ from the reference program's by a relative error of at most 0.0056.
Values may be sent and summed in bfloat16 or wider, within the bound.
No kernel may reach another device: no remote copies, remote signals or barrier semaphores. Data moves between devices by JAX's collectives and lax.ppermute only.
A program may use at most 64 MiB of HBM per device.

```python
import jax
import jax.numpy as jnp

D = 8192
VALUE_FEATURES = 512
ADAPTER_RANK = 64
TOK_DEV = 216
ADAPTER_COUNT = 2
SLOT = 144
TOKENS = 3456


def draw_adapter_ids(key, part):
    blocks = TOKENS // TOK_DEV
    groups = blocks // ADAPTER_COUNT
    others = ADAPTER_COUNT - 1
    spare = TOK_DEV - SLOT
    base_count = spare // others
    extra = spare - base_count * others
    reach = max(0, min(SLOT - base_count - 1, base_count - 1))
    pairs = others // 2
    key_hot, key_move, key_perm = jax.random.split(key, 3)
    hottest = jnp.repeat(jax.random.randint(key_hot, (groups,), 0, ADAPTER_COUNT), ADAPTER_COUNT)
    counts = base_count + (jnp.arange(others, dtype=jnp.int32) < extra).astype(jnp.int32)
    counts = jnp.broadcast_to(counts, (blocks, others))
    moves = jax.random.randint(key_move, (blocks, pairs), 0, reach + 1)
    shifts = jnp.zeros((blocks, others), jnp.int32)
    shifts = shifts.at[:, 0:2 * pairs:2].add(moves)
    shifts = shifts.at[:, 1:2 * pairs:2].add(-moves)
    counts = jnp.concatenate([jnp.full((blocks, 1), SLOT, jnp.int32), counts + shifts], axis=1)
    bounds = jnp.cumsum(counts, axis=1)
    places = jnp.arange(TOK_DEV, dtype=jnp.int32)
    ordinal = jnp.sum((places[None, :, None] >= bounds[:, None, :]).astype(jnp.int32), axis=2)
    labels = (hottest[:, None] + ordinal) % ADAPTER_COUNT
    block_keys = jax.random.split(key_perm, blocks)

    def shuffle_one(single_key):
        return jax.random.permutation(single_key, TOK_DEV)
    shuffles = jax.vmap(shuffle_one)(block_keys)
    return jnp.take_along_axis(labels, shuffles, axis=1).reshape(TOKENS).astype(jnp.int32)


def shard_levels(stream_key, shape, pieces, low, top_value):
    def one(axis_at, parts):
        draws = jax.random.uniform(jax.random.fold_in(jax.random.fold_in(stream_key, 6), axis_at), (parts,), jnp.float32, low / len(pieces), top_value / len(pieces))
        return jnp.repeat(jnp.exp(draws), shape[axis_at] // parts).reshape((-1,) + (1,) * (len(shape) - axis_at - 1))

    gain = one(*pieces[0])
    for cut in pieces[1:]:
        gain = gain * one(*cut)
    return gain


def normal_values(stream_key, dims, scale, most, shards=(), held_as=jnp.bfloat16):
    factor_of = shard_levels(stream_key, dims, shards, -0.22, 0.18) if shards else 1.0
    array = jax.random.normal(stream_key, dims, jnp.float32) * scale * factor_of
    return jnp.minimum(jnp.maximum(array, -most), most).astype(held_as)


def setup_inputs(seed: int = 0) -> dict:
    splits = jax.random.split(jax.random.key(seed), 7)
    tokens = normal_values(splits[0], (TOKENS, D), 1.0, 6.0, ((0, 16),))
    base_weight = normal_values(splits[1], (D, VALUE_FEATURES), D ** -0.5, 0.0625, ((0, 8), (1, 2)))
    adapter_a = normal_values(splits[2], (ADAPTER_COUNT, ADAPTER_RANK, D), D ** -0.5, 0.0625, ((0, 2),))
    adapter_b = normal_values(splits[3], (ADAPTER_COUNT, ADAPTER_RANK, VALUE_FEATURES), ADAPTER_RANK ** -0.5, 0.75, ((0, 2), (2, 2)))
    cotangent = normal_values(splits[4], (TOKENS, VALUE_FEATURES), (TOKENS // ADAPTER_COUNT) ** -0.5, 0.15625, ((0, 16), (1, 2)))
    adapter_ids = draw_adapter_ids(jax.random.fold_in(splits[6], 71), 0)
    return dict(tokens=tokens, base_weight=base_weight, adapter_a=adapter_a, adapter_b=adapter_b, cotangent=cotangent, adapter_ids=adapter_ids)


adapter_scale = 2.0


def reference(tokens, base_weight, adapter_a, adapter_b, cotangent, adapter_ids):
    base = jnp.dot(tokens, base_weight, preferred_element_type=jnp.float32)
    flat_a = adapter_a.reshape(ADAPTER_COUNT * ADAPTER_RANK, D)
    flattened_up = adapter_b.reshape(ADAPTER_COUNT * ADAPTER_RANK, VALUE_FEATURES)
    selected = adapter_ids[:, None] == jnp.arange(ADAPTER_COUNT, dtype=jnp.int32)[None, :]
    widened = jnp.repeat(selected, ADAPTER_RANK, axis=1)
    low_all = jnp.dot(tokens, flat_a.T, preferred_element_type=jnp.float32)
    rank_activations = jnp.where(widened, low_all, jnp.zeros_like(low_all)).astype(jnp.bfloat16)
    value_update = (adapter_scale * jnp.dot(rank_activations, flattened_up, preferred_element_type=jnp.float32)).astype(jnp.bfloat16)
    projected = (base + value_update.astype(jnp.float32)).astype(jnp.bfloat16)
    backward_full = adapter_scale * jnp.dot(cotangent, flattened_up.T, preferred_element_type=jnp.float32)
    backward_rows = jnp.where(widened, backward_full, jnp.zeros_like(backward_full)).astype(jnp.bfloat16)
    up_gradient = (adapter_scale * jnp.dot(rank_activations.T, cotangent, preferred_element_type=jnp.float32)).reshape(ADAPTER_COUNT, ADAPTER_RANK, VALUE_FEATURES)
    grad_a = jnp.dot(backward_rows.T, tokens, preferred_element_type=jnp.float32).reshape(ADAPTER_COUNT, ADAPTER_RANK, D)
    return projected, grad_a, up_gradient
```

```python
import jax
import jax.numpy as jnp
from jax import lax
from jax.sharding import PartitionSpec as P

adapter_scale = 2.0


def reduce_over_rows(left, right):
    return lax.dot_general(
        left, right, (((0,), (0,)), ((), ())), preferred_element_type=jnp.float32
    )


def contract_cols(left, right):
    return lax.dot_general(
        left, right, (((1,), (1,)), ((), ())), preferred_element_type=jnp.float32
    )


def matmul(left, right):
    return jnp.dot(left, right, preferred_element_type=jnp.float32)


def by_owner(tokens, base_weight, adapter_a, adapter_b, cotangent, adapter_ids):
    owners = lax.axis_size("adapter")
    cores = lax.axis_size("mp")
    token_count, width = tokens.shape
    slot_rows = 4 * token_count // (3 * owners)
    column_part = width // cores
    member = lax.axis_index("mp")
    owner_ids = jnp.arange(owners, dtype=jnp.int32)
    onehot = (adapter_ids[:, None] == owner_ids[None, :]).astype(jnp.int32)
    ranking = jnp.sum((jnp.cumsum(onehot, axis=0) - 1) * onehot, axis=1)
    target = adapter_ids * slot_rows + ranking

    def exchange(rows):
        there = lax.all_to_all(
            rows.reshape(owners, slot_rows, rows.shape[1]),
            "adapter",
            split_axis=0,
            concat_axis=0,
            tiled=True,
        )
        return there.reshape(owners * slot_rows, rows.shape[1])

    def slotted(rows):
        return jnp.zeros((owners * slot_rows, rows.shape[1]), rows.dtype).at[target].set(rows)

    arrived = exchange(slotted(tokens))
    incoming_gradient = exchange(slotted(cotangent))
    own_a = adapter_a[0]
    own_b = adapter_b[0]
    feature_cols = lax.dynamic_slice_in_dim(arrived, member * column_part, column_part, 1)
    low = contract_cols(arrived, own_a).astype(jnp.bfloat16)
    value_update = (adapter_scale * matmul(low, own_b)).astype(jnp.bfloat16)
    delta_tokens = exchange(value_update)[target]
    base = matmul(tokens, lax.all_gather(base_weight, "dp", axis=0, tiled=True))
    projected = (base + delta_tokens.astype(jnp.float32)).astype(jnp.bfloat16)
    backward_total = lax.psum(contract_cols(incoming_gradient, own_b), "mp")
    backward_rows = (adapter_scale * backward_total).astype(jnp.bfloat16)
    up_term = adapter_scale * reduce_over_rows(low, incoming_gradient)
    term_a = reduce_over_rows(backward_rows, feature_cols)
    return (
        projected,
        lax.psum_scatter(term_a[None], "dp", scatter_dimension=1, tiled=True),
        lax.psum_scatter(up_term[None], "dp", scatter_dimension=1, tiled=True),
    )


AXES = ("dp", "adapter", "mp")


def by_width(tokens, base_weight, adapter_a, adapter_b, cotangent, adapter_ids):
    members = lax.axis_size("dp")
    line = members // 2
    half = line // 2
    count, width = tokens.shape
    features = cotangent.shape[1]
    rank = adapter_a.shape[1]
    block = width // (4 * line)
    part = half * block
    rows = rank // members
    expanded = 2 * rank
    padded = count + 8

    d = lax.axis_index("dp")
    z, x = d // 2, d % 2
    y = lax.axis_index("adapter")
    c = lax.axis_index("mp")

    def swap(array, dz=0, dx=0, dy=0, dc=0):
        pairs = []
        for here in range(members * 4):
            at_z, at_x, at_y, at_c = here // 8, here // 4 % 2, here // 2 % 2, here % 2
            there = (((at_z ^ dz) * 2 + (at_x ^ dx)) * 2 + (at_y ^ dy)) * 2 + (at_c ^ dc)
            pairs.append((here, there))
        return lax.ppermute(array, AXES, pairs)

    def columns(array, core, side, owner):
        return jnp.concatenate(
            [
                lax.dynamic_slice_in_dim(
                    array, (((core * half + j) * 2 + side) * 2 + owner) * block, block, 1
                )
                for j in range(half)
            ],
            axis=1,
        )

    own_a, own_b = adapter_a[0], adapter_b[0]
    part_x = swap(columns(tokens, c, 1 - x, y), dx=1)
    part_y = swap(
        jnp.concatenate([columns(tokens, c, x, 1 - y), columns(own_a, c, x, 1 - y)], axis=0), dy=1
    )
    part_d = swap(columns(tokens, c, 1 - x, 1 - y), dx=1, dy=1)
    id_rows = jnp.broadcast_to(
        jnp.pad(adapter_ids.astype(jnp.bfloat16), (0, features - count))[None], (8, features)
    )
    own_grads = jnp.concatenate([cotangent, id_rows], axis=0)
    grads_y = swap(jnp.concatenate([own_grads, own_b], axis=0), dy=1)
    grads_x = swap(own_grads, dx=1)
    grads_d = swap(own_grads, dx=1, dy=1)
    own_weight = lax.dynamic_slice_in_dim(base_weight, y * block, block, 0)
    weights = [own_weight] + [swap(own_weight, dz=k) for k in range(1, line)]

    grads = jnp.concatenate(
        [own_grads, grads_x, grads_y[:padded], grads_d, own_b, grads_y[padded:]], axis=0
    )
    grads_other = swap(grads, dc=1)

    def interleave(mine, theirs):
        owner = lax.broadcasted_iota(jnp.int32, (members, 2, rows, mine.shape[1]), 1)
        return jnp.where(
            owner == y, mine.reshape(members, 1, rows, -1), theirs.reshape(members, 1, rows, -1)
        ).reshape(expanded, -1)

    tail = 4 * padded
    up_here = interleave(grads[tail : tail + rank], grads[tail + rank :])
    up_other = interleave(grads_other[tail : tail + rank], grads_other[tail + rank :])
    owner_of_row = lax.broadcasted_iota(jnp.int32, (expanded, 1), 0) // rows % 2
    masks = [
        grads[s * padded + count, :count][None] == owner_of_row.astype(jnp.bfloat16)
        for s in range(4)
    ]
    back_sum = contract_cols(up_here, grads[:tail]) + contract_cols(up_other, grads_other[:tail])
    back = [
        jnp.where(
            masks[s], adapter_scale * back_sum[:, s * padded : s * padded + count], 0.0
        ).astype(jnp.bfloat16)
        for s in range(4)
    ]

    other_x, other_y, other_d = (swap(p, dc=1) for p in (part_x, part_y, part_d))
    here = [columns(tokens, c, x, y), part_x, part_y[:count], part_d]
    other = [columns(tokens, 1 - c, x, y), other_x, other_y[:count], other_d]
    down_here = interleave(columns(own_a, c, x, y), part_y[count:])
    down_other = interleave(columns(own_a, 1 - c, x, y), other_y[count:])

    grad_sum = 0.0
    up_sum = 0.0
    lows = []
    for s in range(4):
        grad_sum += matmul(back[s], here[s])
        low = contract_cols(down_here, here[s]) + contract_cols(down_other, other[s])
        low = adapter_scale * jnp.where(masks[s], low, 0.0)
        high = low.astype(jnp.bfloat16)
        rest = (low - high.astype(jnp.float32)).astype(jnp.bfloat16)
        lows.append((high, rest))
        up_sum += matmul(high, grads[s * padded : s * padded + count])

    terms = jnp.concatenate([grad_sum, up_sum], axis=1).astype(jnp.bfloat16)
    gathered = lax.all_to_all(terms, ("dp", "adapter"), split_axis=0, concat_axis=0, tiled=True)
    gathered = gathered.reshape(line, 2, 2, rows, part + features)
    total = jnp.sum(gathered.astype(jnp.float32), axis=0)
    up_gradient = jnp.sum(total[..., part:], axis=(0, 1))[None]
    grad_a = jnp.concatenate(
        [
            total[side, owner, :, j * block : (j + 1) * block]
            for j in range(half)
            for side in range(2)
            for owner in range(2)
        ],
        axis=1,
    )[None]

    flip_half, flip_low = (z // half) ^ c, z % half

    def pick(j, flip):
        index = flip * half + (flip_low ^ j)
        chosen = weights[0]
        for k in range(1, line):
            chosen = jnp.where(index == k, weights[k], chosen)
        return chosen

    weight_here = jnp.concatenate([pick(j, flip_half) for j in range(half)], axis=0)
    weight_other = jnp.concatenate([pick(j, 1 - flip_half) for j in range(half)], axis=0)
    values = []
    for s in range(4):
        high, rest = lows[s]
        values.append(
            matmul(here[s], weight_here)
            + matmul(other[s], weight_other)
            + reduce_over_rows(high, up_here)
            + reduce_over_rows(rest, up_here)
        )
    projected = (
        values[0]
        + swap(values[1].astype(jnp.bfloat16), dx=1).astype(jnp.float32)
        + swap(values[2].astype(jnp.bfloat16), dy=1).astype(jnp.float32)
        + swap(values[3].astype(jnp.bfloat16), dx=1, dy=1).astype(jnp.float32)
    ).astype(jnp.bfloat16)
    return projected, grad_a, up_gradient


def solution(mesh):
    line = mesh.shape["dp"] // 2
    square = mesh.shape["adapter"] == 2 and mesh.shape["mp"] == 2 and mesh.shape["dp"] % 4 == 0
    return jax.shard_map(
        by_width if square and line & (line - 1) == 0 else by_owner,
        mesh=mesh,
        in_specs=(
            P(("dp", "adapter"), None),
            P("dp", "mp"),
            P("adapter", None, None),
            P("adapter", None, "mp"),
            P(("dp", "adapter"), "mp"),
            P(("dp", "adapter")),
        ),
        out_specs=(P(("dp", "adapter"), "mp"), P("adapter", "dp", "mp"), P("adapter", "dp", "mp")),
        check_vma=False,
    )
```

```python
import functools

import jax
import jax.numpy as jnp
from jax import lax
from jax.experimental import pallas as pl
from jax.experimental.pallas import tpu as pltpu
from jax.sharding import PartitionSpec as P

adapter_scale = 2.0


def reduce_over_rows(left, right):
    return lax.dot_general(
        left, right, (((0,), (0,)), ((), ())), preferred_element_type=jnp.float32
    )


def contract_cols(left, right):
    return lax.dot_general(
        left, right, (((1,), (1,)), ((), ())), preferred_element_type=jnp.float32
    )


def matmul(left, right):
    return jnp.dot(left, right, preferred_element_type=jnp.float32)


def by_owner(tokens, base_weight, adapter_a, adapter_b, cotangent, adapter_ids):
    owners = lax.axis_size("adapter")
    cores = lax.axis_size("mp")
    token_count, width = tokens.shape
    slot_rows = 4 * token_count // (3 * owners)
    column_part = width // cores
    member = lax.axis_index("mp")
    owner_ids = jnp.arange(owners, dtype=jnp.int32)
    onehot = (adapter_ids[:, None] == owner_ids[None, :]).astype(jnp.int32)
    ranking = jnp.sum((jnp.cumsum(onehot, axis=0) - 1) * onehot, axis=1)
    target = adapter_ids * slot_rows + ranking

    def exchange(rows):
        there = lax.all_to_all(
            rows.reshape(owners, slot_rows, rows.shape[1]),
            "adapter",
            split_axis=0,
            concat_axis=0,
            tiled=True,
        )
        return there.reshape(owners * slot_rows, rows.shape[1])

    def slotted(rows):
        return jnp.zeros((owners * slot_rows, rows.shape[1]), rows.dtype).at[target].set(rows)

    arrived = exchange(slotted(tokens))
    incoming_gradient = exchange(slotted(cotangent))
    own_a = adapter_a[0]
    own_b = adapter_b[0]
    feature_cols = lax.dynamic_slice_in_dim(arrived, member * column_part, column_part, 1)
    low = contract_cols(arrived, own_a).astype(jnp.bfloat16)
    value_update = (adapter_scale * matmul(low, own_b)).astype(jnp.bfloat16)
    delta_tokens = exchange(value_update)[target]
    base = matmul(tokens, lax.all_gather(base_weight, "dp", axis=0, tiled=True))
    projected = (base + delta_tokens.astype(jnp.float32)).astype(jnp.bfloat16)
    backward_total = lax.psum(contract_cols(incoming_gradient, own_b), "mp")
    backward_rows = (adapter_scale * backward_total).astype(jnp.bfloat16)
    up_term = adapter_scale * reduce_over_rows(low, incoming_gradient)
    term_a = reduce_over_rows(backward_rows, feature_cols)
    return (
        projected,
        lax.psum_scatter(term_a[None], "dp", scatter_dimension=1, tiled=True),
        lax.psum_scatter(up_term[None], "dp", scatter_dimension=1, tiled=True),
    )


AXES = ("dp", "adapter", "mp")
HBM = pl.BlockSpec(memory_space=pl.ANY)
VMEM = pl.BlockSpec(memory_space=pltpu.VMEM)


def like(shape, dtype):
    return jax.ShapeDtypeStruct(shape, dtype)


def call(kernel, outs, args, scratch=(), held=(), kept=None):
    return pl.pallas_call(
        kernel,
        out_shape=outs,
        in_specs=[VMEM if k in held else HBM for k in range(len(args))],
        out_specs=[VMEM if kept is None or k in kept else HBM for k in range(len(outs))],
        scratch_shapes=scratch,
        compiler_params=pltpu.CompilerParams(vmem_limit_bytes=61 << 20),
        cost_estimate=pl.CostEstimate(flops=1000, bytes_accessed=1000, transcendentals=0),
    )(*args)


def column_blocks(core, side, owner, half, block):
    first = ((core * half * 2 + side) * 2 + owner) * block
    return [pl.multiple_of(first + 4 * j * block, block) for j in range(half)]


def through(moves, stages, sems):
    ins, outs = [], []
    for k, (source, target) in enumerate(moves):
        ins.append(pltpu.make_async_copy(source, stages[k], sems.at[0, k]))
        outs.append(pltpu.make_async_copy(stages[k], target, sems.at[1, k]))
    return ins, outs


def coordinates():
    return lax.axis_index("dp") % 2, lax.axis_index("adapter"), lax.axis_index("mp")


def pack_first(block, tokens, ids, own_b, cotangent, out_x, out_grads, stage, grads, sems, last):
    x, y, c = coordinates()
    count, part = out_x.shape
    half = part // block
    padded = count + 8
    moves = [
        (tokens.at[:, pl.ds(start, block)], out_x.at[:, pl.ds(j * block, block)])
        for j, start in enumerate(column_blocks(c, 1 - x, y, half, block))
    ]
    copies = [
        pltpu.make_async_copy(cotangent, grads.at[pl.ds(0, count)], last.at[0]),
        pltpu.make_async_copy(own_b, grads.at[pl.ds(padded, own_b.shape[0])], last.at[1]),
    ]
    ins, outs = through(moves, [stage.at[j] for j in range(half)], sems)
    for copy in copies + ins:
        copy.start()
    grads[count:padded, :count] = (
        jnp.broadcast_to(ids[...], (8, count)).astype(jnp.float32).astype(grads.dtype)
    )
    grads[count:padded, count:] = jnp.zeros((8, grads.shape[1] - count), grads.dtype)
    for copy in copies:
        copy.wait()
    send = pltpu.make_async_copy(grads, out_grads, last.at[2])
    send.start()
    for arrive, leave in zip(ins, outs):
        arrive.wait()
        leave.start()
    for copy in outs + [send]:
        copy.wait()


def pack_rest(
    block, tokens, own_a, out_y, out_d, out_here, out_other, down_here, down_other, stage, small, sems
):
    x, y, c = coordinates()
    count, part = out_d.shape
    rank = own_a.shape[0]
    half = part // block
    moves, stages = [], []
    for target, place in (
        (out_y, (c, x, 1 - y)),
        (out_d, (c, 1 - x, 1 - y)),
        (out_here, (c, x, y)),
        (out_other, (1 - c, x, y)),
    ):
        for j, start in enumerate(column_blocks(*place, half, block)):
            columns = pl.ds(j * block, block)
            stages.append(stage.at[len(stages)])
            moves.append((tokens.at[:, pl.ds(start, block)], target.at[pl.ds(0, count), columns]))
    used = 0
    for target, offset, place in (
        (out_y, count, (c, x, 1 - y)),
        (down_here, 0, (c, x, y)),
        (down_other, 0, (1 - c, x, y)),
    ):
        for j, start in enumerate(column_blocks(*place, half, block)):
            columns = pl.ds(j * block, block)
            stages.append(small.at[used])
            used += 1
            moves.append((own_a.at[:, pl.ds(start, block)], target.at[pl.ds(offset, rank), columns]))
    ins, outs = through(moves, stages, sems)
    for copy in ins:
        copy.start()
    for arrive, leave in zip(ins, outs):
        arrive.wait()
        leave.start()
    for copy in outs:
        copy.wait()


def source_terms(down_here, down_other, here, other, back, mask, grads):
    low = mask * (contract_cols(down_here, here) + contract_cols(down_other, other))
    high = low.astype(jnp.bfloat16)
    rest = (low - high.astype(jnp.float32)).astype(jnp.bfloat16)
    return matmul(back, here), matmul(high, grads), high, rest


def value_of(here, other, weight, part, high, rest, up):
    c = lax.axis_index("mp")
    return (
        matmul(here, weight[pl.ds(pl.multiple_of(c * part, part), part)])
        + matmul(other, weight[pl.ds(pl.multiple_of((1 - c) * part, part), part)])
        + reduce_over_rows(high, up)
        + reduce_over_rows(rest, up)
    )


def fetch(sources, targets, sems):
    waits, k = [], 0
    for source, target in zip(sources, targets):
        columns = source.shape[1]
        pair = []
        for part in (pl.ds(0, columns // 2), pl.ds(columns // 2, columns // 2)):
            pair.append(pltpu.make_async_copy(source.at[:, part], target.at[:, part], sems.at[k]))
            k += 1
            pair[-1].start()
        waits.append(pair)
    return waits


def wait_all(waits):
    for pair in waits:
        for copy in pair:
            copy.wait()


def terms_kernel(count, rows, *refs):
    ins, refs = refs[:16], refs[16:]
    terms, highs, rests, up_map = refs[:4]
    held, sums, sems = refs[4:20], refs[20], refs[21]
    waits = fetch(ins, held, sems)
    own, over_y, over_x, own2, over_y2, over_x2 = held[:6]
    part = held[6].shape[1]
    rank = terms.shape[0] // 2
    padded = count + 8
    wait_all(waits[:6])
    grads = [own[:padded], over_x[:padded], over_y[:padded], over_x[padded:]]
    grads2 = [own2[:padded], over_x2[:padded], over_y2[:padded], over_x2[padded:]]
    up_map[...] = jnp.concatenate([own[padded:], over_y[padded:]], axis=0)
    up = up_map[...]
    up2 = jnp.concatenate([own2[padded:], over_y2[padded:]], axis=0)
    mine = lax.broadcasted_iota(jnp.int32, (2 * rank, count), 0) < rank
    owner = lax.axis_index("adapter").astype(jnp.float32)
    backs, masks = [], []
    for s in range(4):
        ids = grads[s][count:].astype(jnp.float32)[:1, :count]
        same = jnp.where(ids == owner, adapter_scale, 0.0)
        mask = jnp.where(mine, same, adapter_scale - same)
        both = contract_cols(up, grads[s]) + contract_cols(up2, grads2[s])
        backs.append((mask * both[:, :count]).astype(jnp.bfloat16))
        masks.append(mask)
    wait_all(waits[6:])
    here, other = held[6:14:2], held[7:14:2]
    down_here = jnp.concatenate([held[14][...], here[2][count:]], axis=0)
    down_other = jnp.concatenate([held[15][...], other[2][count:]], axis=0)
    for s in range(4):
        grad, gained, highs[s], rests[s] = source_terms(
            down_here,
            down_other,
            here[s][:count],
            other[s][:count],
            backs[s],
            masks[s],
            grads[s][:count],
        )
        if s == 0:
            sums[:, :part] = grad
            sums[:, part:] = gained
        else:
            sums[:, :part] += grad
            sums[:, part:] += gained
    first = lax.axis_index("adapter") == 0
    for m in range(rank // rows):
        mine, theirs = sums[m * rows : (m + 1) * rows], sums[rank + m * rows : rank + (m + 1) * rows]
        terms[2 * m * rows : 2 * (m + 1) * rows] = jnp.concatenate(
            [jnp.where(first, mine, theirs), jnp.where(first, theirs, mine)], axis=0
        ).astype(terms.dtype)


def values_kernel(count, *refs):
    ins, (highs, rests, up) = refs[:9], refs[9:12]
    values, held, sems = refs[12:16], refs[16:25], refs[25]
    waits = fetch(ins, held, sems)
    wait_all(waits[:1])
    weight = held[0]
    for s in (1, 2, 3, 0):
        wait_all(waits[1 + 2 * s : 3 + 2 * s])
        here, other = held[1 + 2 * s], held[2 + 2 * s]
        values[s][...] = value_of(
            here[:count], other[:count], weight, here.shape[1], highs[s], rests[s], up[...]
        ).astype(values[s].dtype)


def by_width(tokens, base_weight, adapter_a, adapter_b, cotangent, adapter_ids):
    members = lax.axis_size("dp")
    line = members // 2
    half = line // 2
    count, width = tokens.shape
    features = cotangent.shape[1]
    rank = adapter_a.shape[1]
    block = width // (4 * line)
    part = half * block
    rows = rank // members
    padded = count + 8
    bf16, f32 = jnp.bfloat16, jnp.float32
    y = lax.axis_index("adapter")

    def swap(array, dx=0, dy=0, dc=0):
        pairs = []
        for here in range(members * 4):
            at_z, at_x, at_y, at_c = here // 8, here // 4 % 2, here // 2 % 2, here % 2
            there = ((at_z * 2 + (at_x ^ dx)) * 2 + (at_y ^ dy)) * 2 + (at_c ^ dc)
            pairs.append((here, there))
        return lax.ppermute(array, AXES, pairs)

    own_a, own_b = adapter_a[0], adapter_b[0]
    send_x, grads_own = call(
        functools.partial(pack_first, block),
        (like((count, part), bf16), like((padded + rank, features), bf16)),
        (tokens, adapter_ids[None], own_b, cotangent),
        scratch=[
            pltpu.VMEM((half, count, block), bf16),
            pltpu.VMEM((padded + rank, features), bf16),
            pltpu.SemaphoreType.DMA((2, half)),
            pltpu.SemaphoreType.DMA((3,)),
        ],
        held=(1,),
        kept=(),
    )
    own_a, send_x = lax.optimization_barrier((own_a, send_x))
    send_y, send_d, here_own, other_own, down_here, down_other = call(
        functools.partial(pack_rest, block),
        (like((count + rank, part), bf16),)
        + (like((count, part), bf16),) * 3
        + (like((rank, part), bf16),) * 2,
        (tokens, own_a),
        scratch=[
            pltpu.VMEM((4 * half, count, block), bf16),
            pltpu.VMEM((3 * half, rank, block), bf16),
            pltpu.SemaphoreType.DMA((2, 7 * half)),
        ],
        kept=(),
    )
    grads_y = swap(grads_own, dy=1)
    grads_y, send_y = lax.optimization_barrier((grads_y, send_y))
    part_x, part_y = swap(send_x, dx=1), swap(send_y, dy=1)
    own_weight = lax.dynamic_slice_in_dim(base_weight, y * block, block, 0)
    part_x, send_d, grads_y = lax.optimization_barrier((part_x, send_d, grads_y))
    grads_x = swap(jnp.concatenate([grads_own[:padded], grads_y[:padded]], axis=0), dx=1)
    part_d = swap(send_d, dx=1, dy=1)
    part_x, part_y, grads_x = lax.optimization_barrier((part_x, part_y, grads_x))
    weight = lax.all_to_all(
        jnp.tile(own_weight, (line, 1)),
        "dp",
        split_axis=0,
        concat_axis=0,
        tiled=True,
        axis_index_groups=[[2 * k + side for k in range(line)] for side in range(2)],
    )
    grads_pairs = [grads_own, grads_y, grads_x]
    grads_pairs += [swap(array, dc=1) for array in grads_pairs]
    other_x, other_y = swap(part_x, dc=1), swap(part_y, dc=1)
    part_d, other_x, other_y, *grads_pairs = lax.optimization_barrier(
        (part_d, other_x, other_y, *grads_pairs)
    )
    parts = (here_own, other_own, part_x, other_x, part_y, other_y, part_d, swap(part_d, dc=1))
    args = (*grads_pairs, *parts, down_here, down_other)
    terms, highs, rests, up_map = call(
        functools.partial(terms_kernel, count, rows),
        (
            like((2 * rank, part + features), bf16),
            like((4, 2 * rank, count), bf16),
            like((4, 2 * rank, count), bf16),
            like((2 * rank, features), bf16),
        ),
        args,
        scratch=[pltpu.VMEM(arg.shape, arg.dtype) for arg in args]
        + [
            pltpu.VMEM((2 * rank, part + features), f32),
            pltpu.SemaphoreType.DMA((2 * len(args),)),
        ],
    )
    gathered = lax.all_to_all(terms, ("dp", "adapter"), split_axis=0, concat_axis=0, tiled=True)
    gathered = gathered.reshape(line, 2, 2, rows, part + features)
    sums = jnp.sum(gathered.astype(f32), axis=0)
    up_gradient = jnp.sum(sums[..., part:], axis=(0, 1))[None]
    grad_a = jnp.concatenate(
        [
            sums[side, owner, :, j * block : (j + 1) * block]
            for j in range(half)
            for side in range(2)
            for owner in range(2)
        ],
        axis=1,
    )[None]
    args = (weight, *parts)
    value, value_x, value_y, value_d = call(
        functools.partial(values_kernel, count),
        (like((count, features), f32),) + (like((count, features), bf16),) * 3,
        args + (highs, rests, up_map),
        scratch=[pltpu.VMEM(arg.shape, arg.dtype) for arg in args]
        + [pltpu.SemaphoreType.DMA((2 * len(args),))],
        held=(9, 10, 11),
    )
    projected = (
        value
        + swap(value_x, dx=1).astype(f32)
        + swap(value_y, dy=1).astype(f32)
        + swap(value_d, dx=1, dy=1).astype(f32)
    ).astype(bf16)
    return projected, grad_a, up_gradient


def solution(mesh):
    line = mesh.shape["dp"] // 2
    square = mesh.shape["adapter"] == 2 and mesh.shape["mp"] == 2 and mesh.shape["dp"] % 4 == 0
    return jax.shard_map(
        by_width if square and line & (line - 1) == 0 else by_owner,
        mesh=mesh,
        in_specs=(
            P(("dp", "adapter"), None),
            P("dp", "mp"),
            P("adapter", None, None),
            P("adapter", None, "mp"),
            P(("dp", "adapter"), "mp"),
            P(("dp", "adapter")),
        ),
        out_specs=(P(("dp", "adapter"), "mp"), P("adapter", "dp", "mp"), P("adapter", "dp", "mp")),
        check_vma=False,
    )
```

```python
import functools

import jax
import jax.numpy as jnp
from jax import lax
from jax.experimental import pallas as pl
from jax.experimental.pallas import tpu as pltpu
from jax.sharding import PartitionSpec as P

adapter_scale = 2.0


def reduce_over_rows(left, right):
    return lax.dot_general(
        left, right, (((0,), (0,)), ((), ())), preferred_element_type=jnp.float32
    )


def contract_cols(left, right):
    return lax.dot_general(
        left, right, (((1,), (1,)), ((), ())), preferred_element_type=jnp.float32
    )


def matmul(left, right):
    return jnp.dot(left, right, preferred_element_type=jnp.float32)


def by_owner(tokens, base_weight, adapter_a, adapter_b, cotangent, adapter_ids):
    owners = lax.axis_size("adapter")
    cores = lax.axis_size("mp")
    token_count, width = tokens.shape
    slot_rows = 4 * token_count // (3 * owners)
    column_part = width // cores
    member = lax.axis_index("mp")
    owner_ids = jnp.arange(owners, dtype=jnp.int32)
    onehot = (adapter_ids[:, None] == owner_ids[None, :]).astype(jnp.int32)
    ranking = jnp.sum((jnp.cumsum(onehot, axis=0) - 1) * onehot, axis=1)
    target = adapter_ids * slot_rows + ranking

    def exchange(rows):
        there = lax.all_to_all(
            rows.reshape(owners, slot_rows, rows.shape[1]),
            "adapter",
            split_axis=0,
            concat_axis=0,
            tiled=True,
        )
        return there.reshape(owners * slot_rows, rows.shape[1])

    def slotted(rows):
        return jnp.zeros((owners * slot_rows, rows.shape[1]), rows.dtype).at[target].set(rows)

    arrived = exchange(slotted(tokens))
    incoming_gradient = exchange(slotted(cotangent))
    own_a = adapter_a[0]
    own_b = adapter_b[0]
    feature_cols = lax.dynamic_slice_in_dim(arrived, member * column_part, column_part, 1)
    low = contract_cols(arrived, own_a).astype(jnp.bfloat16)
    value_update = (adapter_scale * matmul(low, own_b)).astype(jnp.bfloat16)
    delta_tokens = exchange(value_update)[target]
    base = matmul(tokens, lax.all_gather(base_weight, "dp", axis=0, tiled=True))
    projected = (base + delta_tokens.astype(jnp.float32)).astype(jnp.bfloat16)
    backward_total = lax.psum(contract_cols(incoming_gradient, own_b), "mp")
    backward_rows = (adapter_scale * backward_total).astype(jnp.bfloat16)
    up_term = adapter_scale * reduce_over_rows(low, incoming_gradient)
    term_a = reduce_over_rows(backward_rows, feature_cols)
    return (
        projected,
        lax.psum_scatter(term_a[None], "dp", scatter_dimension=1, tiled=True),
        lax.psum_scatter(up_term[None], "dp", scatter_dimension=1, tiled=True),
    )


AXES = ("dp", "adapter", "mp")
HBM = pl.BlockSpec(memory_space=pl.ANY)
VMEM = pl.BlockSpec(memory_space=pltpu.VMEM)


def like(shape, dtype):
    return jax.ShapeDtypeStruct(shape, dtype)


def call(kernel, outs, args, scratch=(), held=(), kept=None):
    return pl.pallas_call(
        kernel,
        out_shape=outs,
        in_specs=[VMEM if k in held else HBM for k in range(len(args))],
        out_specs=[VMEM if kept is None or k in kept else HBM for k in range(len(outs))],
        scratch_shapes=scratch,
        compiler_params=pltpu.CompilerParams(vmem_limit_bytes=56 << 20),
        cost_estimate=pl.CostEstimate(flops=1000, bytes_accessed=1000, transcendentals=0),
    )(*args)


def column_blocks(core, side, owner, half, block):
    first = ((core * half * 2 + side) * 2 + owner) * block
    return [pl.multiple_of(first + 4 * j * block, block) for j in range(half)]


def through(moves, stages, sems):
    ins, outs = [], []
    for k, (source, target) in enumerate(moves):
        ins.append(pltpu.make_async_copy(source, stages[k], sems.at[0, k]))
        outs.append(pltpu.make_async_copy(stages[k], target, sems.at[1, k]))
    return ins, outs


def coordinates():
    return lax.axis_index("dp") % 2, lax.axis_index("adapter"), lax.axis_index("mp")


def pack_first(block, tokens, ids, own_b, cotangent, out_x, out_grads, stage, grads, sems, last):
    x, y, c = coordinates()
    count, part = out_x.shape
    half = part // block
    padded = count + 8
    moves = [
        (tokens.at[:, pl.ds(start, block)], out_x.at[:, pl.ds(j * block, block)])
        for j, start in enumerate(column_blocks(c, 1 - x, y, half, block))
    ]
    copies = [
        pltpu.make_async_copy(cotangent, grads.at[pl.ds(0, count)], last.at[0]),
        pltpu.make_async_copy(own_b, grads.at[pl.ds(padded, own_b.shape[0])], last.at[1]),
    ]
    ins, outs = through(moves, [stage.at[j] for j in range(half)], sems)
    for copy in copies + ins:
        copy.start()
    grads[count:padded, :count] = (
        jnp.broadcast_to(ids[...], (8, count)).astype(jnp.float32).astype(grads.dtype)
    )
    grads[count:padded, count:] = jnp.zeros((8, grads.shape[1] - count), grads.dtype)
    for copy in copies:
        copy.wait()
    send = pltpu.make_async_copy(grads, out_grads, last.at[2])
    send.start()
    for arrive, leave in zip(ins, outs):
        arrive.wait()
        leave.start()
    for copy in outs + [send]:
        copy.wait()


def pack_rest(
    block, tokens, own_a, out_y, out_d, out_here, out_other, down_here, down_other, stage, small, sems
):
    x, y, c = coordinates()
    count, part = out_d.shape
    rank = own_a.shape[0]
    half = part // block
    moves, stages = [], []
    for target, place in (
        (out_y, (c, x, 1 - y)),
        (out_d, (c, 1 - x, 1 - y)),
        (out_here, (c, x, y)),
        (out_other, (1 - c, x, y)),
    ):
        for j, start in enumerate(column_blocks(*place, half, block)):
            columns = pl.ds(j * block, block)
            stages.append(stage.at[len(stages)])
            moves.append((tokens.at[:, pl.ds(start, block)], target.at[pl.ds(0, count), columns]))
    used = 0
    for target, offset, place in (
        (out_y, count, (c, x, 1 - y)),
        (down_here, 0, (c, x, y)),
        (down_other, 0, (1 - c, x, y)),
    ):
        for j, start in enumerate(column_blocks(*place, half, block)):
            columns = pl.ds(j * block, block)
            stages.append(small.at[used])
            used += 1
            moves.append((own_a.at[:, pl.ds(start, block)], target.at[pl.ds(offset, rank), columns]))
    ins, outs = through(moves, stages, sems)
    for copy in ins:
        copy.start()
    for arrive, leave in zip(ins, outs):
        arrive.wait()
        leave.start()
    for copy in outs:
        copy.wait()


def source_terms(down_here, down_other, here, other, back, mask, grads):
    low = mask * (contract_cols(down_here, here) + contract_cols(down_other, other))
    high = low.astype(jnp.bfloat16)
    rest = (low - high.astype(jnp.float32)).astype(jnp.bfloat16)
    return matmul(back, here), matmul(high, grads), high, rest


def value_of(here, other, weight, part, high, rest, up):
    c = lax.axis_index("mp")
    return (
        matmul(here, weight[pl.ds(pl.multiple_of(c * part, part), part)])
        + matmul(other, weight[pl.ds(pl.multiple_of((1 - c) * part, part), part)])
        + reduce_over_rows(high, up)
        + reduce_over_rows(rest, up)
    )


def fetch(sources, targets, sems):
    copies = [
        pltpu.make_async_copy(source, target, sems.at[k])
        for k, (source, target) in enumerate(zip(sources, targets))
    ]
    for copy in copies:
        copy.start()
    return copies


def wait_all(copies):
    for copy in copies:
        copy.wait()


def early_kernel(count, *refs):
    ins, refs = refs[:14], refs[14:]
    total, highs, rests, up_map, back_d, mask_d, down_here, down_other = refs[:8]
    held, sems = refs[8:22], refs[22]
    waits = fetch(ins, held, sems)
    parts, others = held[6:12], held[:6] + held[12:]
    own, over_y, over_x, own2, over_y2, over_x2 = others[:6]
    part = parts[0].shape[1]
    rank = total.shape[0] // 2
    padded = count + 8
    wait_all(waits[:6])
    grads = [own[:padded], over_x[:padded], over_y[:padded], over_x[padded:]]
    grads2 = [own2[:padded], over_x2[:padded], over_y2[:padded], over_x2[padded:]]
    up_map[...] = jnp.concatenate([own[padded:], over_y[padded:]], axis=0)
    up = up_map[...]
    up2 = jnp.concatenate([own2[padded:], over_y2[padded:]], axis=0)
    mine = lax.broadcasted_iota(jnp.int32, (2 * rank, count), 0) < rank
    owner = lax.axis_index("adapter").astype(jnp.float32)
    backs, masks = [], []
    for s in range(4):
        ids = grads[s][count:].astype(jnp.float32)[:1, :count]
        same = jnp.where(ids == owner, adapter_scale, 0.0)
        mask = jnp.where(mine, same, adapter_scale - same)
        both = contract_cols(up, grads[s]) + contract_cols(up2, grads2[s])
        backs.append((mask * both[:, :count]).astype(jnp.bfloat16))
        masks.append(mask)
    back_d[...] = backs[3]
    mask_d[...] = masks[3]
    wait_all(waits[6:])
    here, other = parts[::2], parts[1::2]
    down_here[...] = jnp.concatenate([others[6][...], here[2][count:]], axis=0)
    down_other[...] = jnp.concatenate([others[7][...], other[2][count:]], axis=0)
    for s in range(3):
        grad, gained, highs[s], rests[s] = source_terms(
            down_here[...],
            down_other[...],
            here[s][:count],
            other[s][:count],
            backs[s],
            masks[s],
            grads[s][:count],
        )
        if s == 0:
            total[:, :part] = grad
            total[:, part:] = gained
        else:
            total[:, :part] += grad
            total[:, part:] += gained


def late_kernel(rows, *refs):
    ins, (terms, high, rest), held, (sums, sems) = refs[:8], refs[8:11], refs[11:19], refs[19:]
    grads, back, mask, down_here, down_other, here, other, total = held
    count, part = here.shape
    wait_all(
        fetch((ins[0].at[pl.ds(grads.shape[0], grads.shape[0])],) + ins[1:], held, sems)
    )
    grad, up, high[...], rest[...] = source_terms(
        down_here[...], down_other[...], here[...], other[...], back[...], mask[...], grads[:count]
    )
    sums[:, :part] = total[:, :part] + grad
    sums[:, part:] = total[:, part:] + up
    rank = sums.shape[0] // 2
    first = lax.axis_index("adapter") == 0
    for m in range(rank // rows):
        mine, theirs = sums[m * rows : (m + 1) * rows], sums[rank + m * rows : rank + (m + 1) * rows]
        terms[2 * m * rows : 2 * (m + 1) * rows] = jnp.concatenate(
            [jnp.where(first, mine, theirs), jnp.where(first, theirs, mine)], axis=0
        ).astype(terms.dtype)


def values_kernel(count, *refs):
    ins, values, held, sems = refs[:14], refs[14:18], refs[18:32], refs[32]
    copies = fetch(ins, held, sems)
    weight, up, highs, rests, high_d, rest_d = held[:6]
    parts = held[6:]
    wait_all(copies[:6])
    for k, s in enumerate((3, 1, 2, 0)):
        wait_all(copies[6 + 2 * k : 8 + 2 * k])
        here, other = parts[2 * k], parts[1 + 2 * k]
        values[s][...] = value_of(
            here[:count],
            other[:count],
            weight,
            here.shape[1],
            high_d[...] if s == 3 else highs[s],
            rest_d[...] if s == 3 else rests[s],
            up[...],
        ).astype(values[s].dtype)


def by_width(tokens, base_weight, adapter_a, adapter_b, cotangent, adapter_ids):
    members = lax.axis_size("dp")
    line = members // 2
    half = line // 2
    count, width = tokens.shape
    features = cotangent.shape[1]
    rank = adapter_a.shape[1]
    block = width // (4 * line)
    part = half * block
    rows = rank // members
    padded = count + 8
    bf16, f32 = jnp.bfloat16, jnp.float32
    y = lax.axis_index("adapter")

    def swap(array, dx=0, dy=0, dc=0):
        pairs = []
        for here in range(members * 4):
            at_z, at_x, at_y, at_c = here // 8, here // 4 % 2, here // 2 % 2, here % 2
            there = ((at_z * 2 + (at_x ^ dx)) * 2 + (at_y ^ dy)) * 2 + (at_c ^ dc)
            pairs.append((here, there))
        return lax.ppermute(array, AXES, pairs)

    own_a, own_b = adapter_a[0], adapter_b[0]
    send_x, grads_own = call(
        functools.partial(pack_first, block),
        (like((count, part), bf16), like((padded + rank, features), bf16)),
        (tokens, adapter_ids[None], own_b, cotangent),
        scratch=[
            pltpu.VMEM((half, count, block), bf16),
            pltpu.VMEM((padded + rank, features), bf16),
            pltpu.SemaphoreType.DMA((2, half)),
            pltpu.SemaphoreType.DMA((3,)),
        ],
        held=(1,),
        kept=(),
    )
    own_a, send_x = lax.optimization_barrier((own_a, send_x))
    send_y, send_d, here_own, other_own, down_here, down_other = call(
        functools.partial(pack_rest, block),
        (like((count + rank, part), bf16),)
        + (like((count, part), bf16),) * 3
        + (like((rank, part), bf16),) * 2,
        (tokens, own_a),
        scratch=[
            pltpu.VMEM((4 * half, count, block), bf16),
            pltpu.VMEM((3 * half, rank, block), bf16),
            pltpu.SemaphoreType.DMA((2, 7 * half)),
        ],
        kept=(),
    )
    grads_y = swap(grads_own, dy=1)
    grads_y, send_y = lax.optimization_barrier((grads_y, send_y))
    part_x, part_y = swap(send_x, dx=1), swap(send_y, dy=1)
    own_weight = lax.dynamic_slice_in_dim(base_weight, y * block, block, 0)
    part_x, send_d, grads_y = lax.optimization_barrier((part_x, send_d, grads_y))
    grads_x = swap(jnp.concatenate([grads_own[:padded], grads_y[:padded]], axis=0), dx=1)
    part_d = swap(send_d, dx=1, dy=1)
    part_x, part_y, grads_x = lax.optimization_barrier((part_x, part_y, grads_x))
    weight = lax.all_to_all(
        jnp.tile(own_weight, (line, 1)),
        "dp",
        split_axis=0,
        concat_axis=0,
        tiled=True,
        axis_index_groups=[[2 * k + side for k in range(line)] for side in range(2)],
    )
    grads = (grads_own, grads_y, grads_x)
    parts = (here_own, other_own, part_x, swap(part_x, dc=1), part_y, swap(part_y, dc=1))
    args = (*grads, *(swap(array, dc=1) for array in grads), *parts, down_here, down_other)
    total, highs, rests, up_map, back_d, mask_d, down_here, down_other = call(
        functools.partial(early_kernel, count),
        (
            like((2 * rank, part + features), f32),
            like((3, 2 * rank, count), bf16),
            like((3, 2 * rank, count), bf16),
            like((2 * rank, features), bf16),
            like((2 * rank, count), bf16),
            like((2 * rank, count), f32),
            like((2 * rank, part), bf16),
            like((2 * rank, part), bf16),
        ),
        args,
        scratch=[pltpu.VMEM(array.shape, array.dtype) for array in args]
        + [pltpu.SemaphoreType.DMA((len(args),))],
    )
    part_d, total = lax.optimization_barrier((part_d, total))
    parts_d = (part_d, swap(part_d, dc=1))
    args = (grads_x, back_d, mask_d, down_here, down_other, *parts_d, total)
    terms, high_d, rest_d = call(
        functools.partial(late_kernel, rows),
        (
            like((2 * rank, part + features), bf16),
            like((2 * rank, count), bf16),
            like((2 * rank, count), bf16),
        ),
        args,
        scratch=[pltpu.VMEM((padded, features), bf16)]
        + [pltpu.VMEM(array.shape, array.dtype) for array in args[1:]]
        + [pltpu.VMEM(total.shape, f32), pltpu.SemaphoreType.DMA((len(args),))],
    )
    gathered = lax.all_to_all(terms, ("dp", "adapter"), split_axis=0, concat_axis=0, tiled=True)
    args = (weight, up_map, highs, rests, high_d, rest_d, *parts_d, *parts[2:], *parts[:2])
    value, value_x, value_y, value_d = call(
        functools.partial(values_kernel, count),
        (like((count, features), f32),) + (like((count, features), bf16),) * 3,
        args,
        scratch=[pltpu.VMEM(array.shape, array.dtype) for array in args]
        + [pltpu.SemaphoreType.DMA((len(args),))],
    )
    value_x, value_y, value_d = swap(value_x, dx=1), swap(value_y, dy=1), swap(value_d, dx=1, dy=1)
    gathered = gathered.reshape(line, 2, 2, rows, part + features)
    sums = jnp.sum(gathered.astype(f32), axis=0)
    up_gradient = jnp.sum(sums[..., part:], axis=(0, 1))[None]
    grad_a = jnp.concatenate(
        [
            sums[side, owner, :, j * block : (j + 1) * block]
            for j in range(half)
            for side in range(2)
            for owner in range(2)
        ],
        axis=1,
    )[None]
    value_x, value_y, value_d, grad_a = lax.optimization_barrier((value_x, value_y, value_d, grad_a))
    projected = (
        value + value_x.astype(f32) + value_y.astype(f32) + value_d.astype(f32)
    ).astype(bf16)
    return projected, grad_a, up_gradient


def solution(mesh):
    line = mesh.shape["dp"] // 2
    square = mesh.shape["adapter"] == 2 and mesh.shape["mp"] == 2 and mesh.shape["dp"] % 4 == 0
    return jax.shard_map(
        by_width if square and line & (line - 1) == 0 else by_owner,
        mesh=mesh,
        in_specs=(
            P(("dp", "adapter"), None),
            P("dp", "mp"),
            P("adapter", None, None),
            P("adapter", None, "mp"),
            P(("dp", "adapter"), "mp"),
            P(("dp", "adapter")),
        ),
        out_specs=(P(("dp", "adapter"), "mp"), P("adapter", "dp", "mp"), P("adapter", "dp", "mp")),
        check_vma=False,
    )
```

```python
import functools

import jax
import jax.numpy as jnp
from jax import lax
from jax.experimental import pallas as pl
from jax.experimental.pallas import tpu as pltpu
from jax.sharding import PartitionSpec as P

adapter_scale = 2.0


def reduce_over_rows(left, right):
    return lax.dot_general(
        left, right, (((0,), (0,)), ((), ())), preferred_element_type=jnp.float32
    )


def contract_cols(left, right):
    return lax.dot_general(
        left, right, (((1,), (1,)), ((), ())), preferred_element_type=jnp.float32
    )


def matmul(left, right):
    return jnp.dot(left, right, preferred_element_type=jnp.float32)


def by_owner(tokens, base_weight, adapter_a, adapter_b, cotangent, adapter_ids):
    owners = lax.axis_size("adapter")
    cores = lax.axis_size("mp")
    token_count, width = tokens.shape
    slot_rows = 4 * token_count // (3 * owners)
    column_part = width // cores
    member = lax.axis_index("mp")
    owner_ids = jnp.arange(owners, dtype=jnp.int32)
    onehot = (adapter_ids[:, None] == owner_ids[None, :]).astype(jnp.int32)
    ranking = jnp.sum((jnp.cumsum(onehot, axis=0) - 1) * onehot, axis=1)
    target = adapter_ids * slot_rows + ranking

    def exchange(rows):
        there = lax.all_to_all(
            rows.reshape(owners, slot_rows, rows.shape[1]),
            "adapter",
            split_axis=0,
            concat_axis=0,
            tiled=True,
        )
        return there.reshape(owners * slot_rows, rows.shape[1])

    def slotted(rows):
        return jnp.zeros((owners * slot_rows, rows.shape[1]), rows.dtype).at[target].set(rows)

    arrived = exchange(slotted(tokens))
    incoming_gradient = exchange(slotted(cotangent))
    own_a = adapter_a[0]
    own_b = adapter_b[0]
    feature_cols = lax.dynamic_slice_in_dim(arrived, member * column_part, column_part, 1)
    low = contract_cols(arrived, own_a).astype(jnp.bfloat16)
    value_update = (adapter_scale * matmul(low, own_b)).astype(jnp.bfloat16)
    delta_tokens = exchange(value_update)[target]
    base = matmul(tokens, lax.all_gather(base_weight, "dp", axis=0, tiled=True))
    projected = (base + delta_tokens.astype(jnp.float32)).astype(jnp.bfloat16)
    backward_total = lax.psum(contract_cols(incoming_gradient, own_b), "mp")
    backward_rows = (adapter_scale * backward_total).astype(jnp.bfloat16)
    up_term = adapter_scale * reduce_over_rows(low, incoming_gradient)
    term_a = reduce_over_rows(backward_rows, feature_cols)
    return (
        projected,
        lax.psum_scatter(term_a[None], "dp", scatter_dimension=1, tiled=True),
        lax.psum_scatter(up_term[None], "dp", scatter_dimension=1, tiled=True),
    )


AXES = ("dp", "adapter", "mp")
HBM = pl.BlockSpec(memory_space=pl.ANY)
VMEM = pl.BlockSpec(memory_space=pltpu.VMEM)


def like(shape, dtype):
    return jax.ShapeDtypeStruct(shape, dtype)


def call(kernel, outs, args, scratch=(), held=(), kept=None):
    return pl.pallas_call(
        kernel,
        out_shape=outs,
        in_specs=[VMEM if k in held else HBM for k in range(len(args))],
        out_specs=[VMEM if kept is None or k in kept else HBM for k in range(len(outs))],
        scratch_shapes=scratch,
        compiler_params=pltpu.CompilerParams(vmem_limit_bytes=56 << 20),
        cost_estimate=pl.CostEstimate(flops=1000, bytes_accessed=1000, transcendentals=0),
    )(*args)


def column_blocks(core, side, owner, half, block):
    first = ((core * half * 2 + side) * 2 + owner) * block
    return [pl.multiple_of(first + 4 * j * block, block) for j in range(half)]


def through(moves, stages, sems):
    ins, outs = [], []
    for k, (source, target) in enumerate(moves):
        ins.append(pltpu.make_async_copy(source, stages[k], sems.at[0, k]))
        outs.append(pltpu.make_async_copy(stages[k], target, sems.at[1, k]))
    return ins, outs


def coordinates():
    return lax.axis_index("dp") % 2, lax.axis_index("adapter"), lax.axis_index("mp")


def pack_first(block, tokens, ids, own_b, cotangent, out_x, out_grads, stage, grads, sems, last):
    x, y, c = coordinates()
    count, part = out_x.shape
    half = part // block
    padded = count + 8
    moves = [
        (tokens.at[:, pl.ds(start, block)], out_x.at[:, pl.ds(j * block, block)])
        for j, start in enumerate(column_blocks(c, 1 - x, y, half, block))
    ]
    copies = [
        pltpu.make_async_copy(cotangent, grads.at[pl.ds(0, count)], last.at[0]),
        pltpu.make_async_copy(own_b, grads.at[pl.ds(padded, own_b.shape[0])], last.at[1]),
    ]
    ins, outs = through(moves, [stage.at[j] for j in range(half)], sems)
    for copy in copies + ins:
        copy.start()
    grads[count:padded, :count] = (
        jnp.broadcast_to(ids[...], (8, count)).astype(jnp.float32).astype(grads.dtype)
    )
    grads[count:padded, count:] = jnp.zeros((8, grads.shape[1] - count), grads.dtype)
    for copy in copies:
        copy.wait()
    send = pltpu.make_async_copy(grads, out_grads, last.at[2])
    send.start()
    for arrive, leave in zip(ins, outs):
        arrive.wait()
        leave.start()
    for copy in outs + [send]:
        copy.wait()


def pack_rest(
    block, tokens, own_a, out_y, out_d, out_here, out_other, down_here, down_other, stage, small, sems
):
    x, y, c = coordinates()
    count, part = out_d.shape
    rank = own_a.shape[0]
    half = part // block
    moves, stages = [], []
    for target, place in (
        (out_y, (c, x, 1 - y)),
        (out_d, (c, 1 - x, 1 - y)),
        (out_here, (c, x, y)),
        (out_other, (1 - c, x, y)),
    ):
        for j, start in enumerate(column_blocks(*place, half, block)):
            columns = pl.ds(j * block, block)
            stages.append(stage.at[len(stages)])
            moves.append((tokens.at[:, pl.ds(start, block)], target.at[pl.ds(0, count), columns]))
    used = 0
    for target, offset, place in (
        (out_y, count, (c, x, 1 - y)),
        (down_here, 0, (c, x, y)),
        (down_other, 0, (1 - c, x, y)),
    ):
        for j, start in enumerate(column_blocks(*place, half, block)):
            columns = pl.ds(j * block, block)
            stages.append(small.at[used])
            used += 1
            moves.append((own_a.at[:, pl.ds(start, block)], target.at[pl.ds(offset, rank), columns]))
    ins, outs = through(moves, stages, sems)
    for copy in ins:
        copy.start()
    for arrive, leave in zip(ins, outs):
        arrive.wait()
        leave.start()
    for copy in outs:
        copy.wait()


def source_terms(down_here, down_other, here, other, back, mask, grads):
    low = mask * (contract_cols(down_here, here) + contract_cols(down_other, other))
    high = low.astype(jnp.bfloat16)
    rest = (low - high.astype(jnp.float32)).astype(jnp.bfloat16)
    return matmul(back, here), matmul(high, grads), high, rest


def value_of(here, other, weight, part, high, rest, up):
    c = lax.axis_index("mp")
    return (
        matmul(here, weight[pl.ds(pl.multiple_of(c * part, part), part)])
        + matmul(other, weight[pl.ds(pl.multiple_of((1 - c) * part, part), part)])
        + reduce_over_rows(high, up)
        + reduce_over_rows(rest, up)
    )


def fetch(sources, targets, sems):
    copies = [
        pltpu.make_async_copy(source, target, sems.at[k])
        for k, (source, target) in enumerate(zip(sources, targets))
    ]
    for copy in copies:
        copy.start()
    return copies


def wait_all(copies):
    for copy in copies:
        copy.wait()


def early_kernel(count, *refs):
    ins, refs = refs[:14], refs[14:]
    total, highs, rests, up_map, back_d, mask_d, down_here, down_other = refs[:8]
    held, sems = refs[8:22], refs[22]
    waits = fetch(ins, held, sems)
    parts, others = held[6:12], held[:6] + held[12:]
    own, over_y, over_x, own2, over_y2, over_x2 = others[:6]
    part = parts[0].shape[1]
    rank = total.shape[0] // 2
    padded = count + 8
    wait_all(waits[:6])
    grads = [own[:padded], over_x[:padded], over_y[:padded], over_x[padded:]]
    grads2 = [own2[:padded], over_x2[:padded], over_y2[:padded], over_x2[padded:]]
    up_map[...] = jnp.concatenate([own[padded:], over_y[padded:]], axis=0)
    up = up_map[...]
    up2 = jnp.concatenate([own2[padded:], over_y2[padded:]], axis=0)
    mine = lax.broadcasted_iota(jnp.int32, (2 * rank, count), 0) < rank
    owner = lax.axis_index("adapter").astype(jnp.float32)
    backs, masks = [], []
    for s in range(4):
        ids = grads[s][count:].astype(jnp.float32)[:1, :count]
        same = jnp.where(ids == owner, adapter_scale, 0.0)
        mask = jnp.where(mine, same, adapter_scale - same)
        both = contract_cols(up, grads[s]) + contract_cols(up2, grads2[s])
        backs.append((mask * both[:, :count]).astype(jnp.bfloat16))
        masks.append(mask)
    back_d[...] = backs[3]
    mask_d[...] = masks[3]
    wait_all(waits[6:])
    here, other = parts[::2], parts[1::2]
    down_here[...] = jnp.concatenate([others[6][...], here[2][count:]], axis=0)
    down_other[...] = jnp.concatenate([others[7][...], other[2][count:]], axis=0)
    for s in range(3):
        grad, gained, highs[s], rests[s] = source_terms(
            down_here[...],
            down_other[...],
            here[s][:count],
            other[s][:count],
            backs[s],
            masks[s],
            grads[s][:count],
        )
        if s == 0:
            total[:, :part] = grad
            total[:, part:] = gained
        else:
            total[:, :part] += grad
            total[:, part:] += gained


def late_kernel(rows, *refs):
    ins, (terms, high, rest), held, (sums, sems) = refs[:8], refs[8:11], refs[11:19], refs[19:]
    grads, back, mask, down_here, down_other, here, other, total = held
    count, part = here.shape
    wait_all(
        fetch((ins[0].at[pl.ds(grads.shape[0], grads.shape[0])],) + ins[1:], held, sems)
    )
    grad, up, high[...], rest[...] = source_terms(
        down_here[...], down_other[...], here[...], other[...], back[...], mask[...], grads[:count]
    )
    sums[:, :part] = total[:, :part] + grad
    sums[:, part:] = total[:, part:] + up
    rank = sums.shape[0] // 2
    first = lax.axis_index("adapter") == 0
    for m in range(rank // rows):
        mine, theirs = sums[m * rows : (m + 1) * rows], sums[rank + m * rows : rank + (m + 1) * rows]
        terms[2 * m * rows : 2 * (m + 1) * rows] = jnp.concatenate(
            [jnp.where(first, mine, theirs), jnp.where(first, theirs, mine)], axis=0
        ).astype(terms.dtype)


def values_kernel(count, *refs):
    ins, values, held, sems = refs[:14], refs[14:18], refs[18:32], refs[32]
    copies = fetch(ins, held, sems)
    weight, up, highs, rests, high_d, rest_d = held[:6]
    parts = held[6:]
    wait_all(copies[:6])
    for k, s in enumerate((3, 1, 2, 0)):
        wait_all(copies[6 + 2 * k : 8 + 2 * k])
        here, other = parts[2 * k], parts[1 + 2 * k]
        values[s][...] = value_of(
            here[:count],
            other[:count],
            weight,
            here.shape[1],
            high_d[...] if s == 3 else highs[s],
            rest_d[...] if s == 3 else rests[s],
            up[...],
        ).astype(values[s].dtype)


def by_width(tokens, base_weight, adapter_a, adapter_b, cotangent, adapter_ids):
    members = lax.axis_size("dp")
    line = members // 2
    half = line // 2
    count, width = tokens.shape
    features = cotangent.shape[1]
    rank = adapter_a.shape[1]
    block = width // (4 * line)
    part = half * block
    rows = rank // members
    padded = count + 8
    bf16, f32 = jnp.bfloat16, jnp.float32
    y = lax.axis_index("adapter")

    def swap(array, dx=0, dy=0, dc=0):
        pairs = []
        for here in range(members * 4):
            at_z, at_x, at_y, at_c = here // 8, here // 4 % 2, here // 2 % 2, here % 2
            there = ((at_z * 2 + (at_x ^ dx)) * 2 + (at_y ^ dy)) * 2 + (at_c ^ dc)
            pairs.append((here, there))
        return lax.ppermute(array, AXES, pairs)

    own_a, own_b = adapter_a[0], adapter_b[0]
    send_x, grads_own = call(
        functools.partial(pack_first, block),
        (like((count, part), bf16), like((padded + rank, features), bf16)),
        (tokens, adapter_ids[None], own_b, cotangent),
        scratch=[
            pltpu.VMEM((half, count, block), bf16),
            pltpu.VMEM((padded + rank, features), bf16),
            pltpu.SemaphoreType.DMA((2, half)),
            pltpu.SemaphoreType.DMA((3,)),
        ],
        held=(1,),
        kept=(),
    )
    own_a, send_x = lax.optimization_barrier((own_a, send_x))
    send_y, send_d, here_own, other_own, down_here, down_other = call(
        functools.partial(pack_rest, block),
        (like((count + rank, part), bf16),)
        + (like((count, part), bf16),) * 3
        + (like((rank, part), bf16),) * 2,
        (tokens, own_a),
        scratch=[
            pltpu.VMEM((4 * half, count, block), bf16),
            pltpu.VMEM((3 * half, rank, block), bf16),
            pltpu.SemaphoreType.DMA((2, 7 * half)),
        ],
        kept=(),
    )
    grads_y = swap(grads_own, dy=1)
    grads_y, send_y = lax.optimization_barrier((grads_y, send_y))
    part_x, part_y = swap(send_x, dx=1), swap(send_y, dy=1)
    own_weight = lax.dynamic_slice_in_dim(base_weight, y * block, block, 0)
    part_x, send_d, grads_y = lax.optimization_barrier((part_x, send_d, grads_y))
    grads_x = swap(jnp.concatenate([grads_own[:padded], grads_y[:padded]], axis=0), dx=1)
    part_d = swap(send_d, dx=1, dy=1)
    part_x, own_again, y_again = lax.optimization_barrier((part_x, grads_own, grads_y))
    grads_own2, grads_y2 = swap(own_again, dc=1), swap(y_again, dc=1)
    part_x, part_y, grads_x, grads_own2, grads_y2 = lax.optimization_barrier(
        (part_x, part_y, grads_x, grads_own2, grads_y2)
    )
    weight = lax.all_to_all(
        jnp.tile(own_weight, (line, 1)),
        "dp",
        split_axis=0,
        concat_axis=0,
        tiled=True,
        axis_index_groups=[[2 * k + side for k in range(line)] for side in range(2)],
    )
    grads = (grads_own, grads_y, grads_x)
    parts = (here_own, other_own, part_x, swap(part_x, dc=1), part_y, swap(part_y, dc=1))
    grads += (grads_own2, grads_y2, swap(grads_x, dc=1))
    args = (*grads, *parts, down_here, down_other)
    total, highs, rests, up_map, back_d, mask_d, down_here, down_other = call(
        functools.partial(early_kernel, count),
        (
            like((2 * rank, part + features), f32),
            like((3, 2 * rank, count), bf16),
            like((3, 2 * rank, count), bf16),
            like((2 * rank, features), bf16),
            like((2 * rank, count), bf16),
            like((2 * rank, count), f32),
            like((2 * rank, part), bf16),
            like((2 * rank, part), bf16),
        ),
        args,
        scratch=[pltpu.VMEM(array.shape, array.dtype) for array in args]
        + [pltpu.SemaphoreType.DMA((len(args),))],
    )
    part_d, total = lax.optimization_barrier((part_d, total))
    parts_d = (part_d, swap(part_d, dc=1))
    args = (grads_x, back_d, mask_d, down_here, down_other, *parts_d, total)
    terms, high_d, rest_d = call(
        functools.partial(late_kernel, rows),
        (
            like((2 * rank, part + features), bf16),
            like((2 * rank, count), bf16),
            like((2 * rank, count), bf16),
        ),
        args,
        scratch=[pltpu.VMEM((padded, features), bf16)]
        + [pltpu.VMEM(array.shape, array.dtype) for array in args[1:]]
        + [pltpu.VMEM(total.shape, f32), pltpu.SemaphoreType.DMA((len(args),))],
    )
    gathered = lax.all_to_all(terms, ("dp", "adapter"), split_axis=0, concat_axis=0, tiled=True)
    args = (weight, up_map, highs, rests, high_d, rest_d, *parts_d, *parts[2:], *parts[:2])
    value, value_x, value_y, value_d = call(
        functools.partial(values_kernel, count),
        (like((count, features), f32),) + (like((count, features), bf16),) * 3,
        args,
        scratch=[pltpu.VMEM(array.shape, array.dtype) for array in args]
        + [pltpu.SemaphoreType.DMA((len(args),))],
    )
    value_x, value_y, value_d = swap(value_x, dx=1), swap(value_y, dy=1), swap(value_d, dx=1, dy=1)
    gathered = gathered.reshape(line, 2, 2, rows, part + features)
    sums = jnp.sum(gathered.astype(f32), axis=0)
    up_gradient = jnp.sum(sums[..., part:], axis=(0, 1))[None]
    grad_a = jnp.concatenate(
        [
            sums[side, owner, :, j * block : (j + 1) * block]
            for j in range(half)
            for side in range(2)
            for owner in range(2)
        ],
        axis=1,
    )[None]
    value_x, value_y, value_d, grad_a = lax.optimization_barrier((value_x, value_y, value_d, grad_a))
    projected = (
        value + value_x.astype(f32) + value_y.astype(f32) + value_d.astype(f32)
    ).astype(bf16)
    return projected, grad_a, up_gradient


def solution(mesh):
    line = mesh.shape["dp"] // 2
    square = mesh.shape["adapter"] == 2 and mesh.shape["mp"] == 2 and mesh.shape["dp"] % 4 == 0
    return jax.shard_map(
        by_width if square and line & (line - 1) == 0 else by_owner,
        mesh=mesh,
        in_specs=(
            P(("dp", "adapter"), None),
            P("dp", "mp"),
            P("adapter", None, None),
            P("adapter", None, "mp"),
            P(("dp", "adapter"), "mp"),
            P(("dp", "adapter")),
        ),
        out_specs=(P(("dp", "adapter"), "mp"), P("adapter", "dp", "mp"), P("adapter", "dp", "mp")),
        check_vma=False,
    )
```

```python
import functools

import jax
import jax.numpy as jnp
from jax import lax
from jax.experimental import pallas as pl
from jax.experimental.pallas import tpu as pltpu
from jax.sharding import PartitionSpec as P

adapter_scale = 2.0


def reduce_over_rows(left, right):
    return lax.dot_general(
        left, right, (((0,), (0,)), ((), ())), preferred_element_type=jnp.float32
    )


def contract_cols(left, right):
    return lax.dot_general(
        left, right, (((1,), (1,)), ((), ())), preferred_element_type=jnp.float32
    )


def matmul(left, right):
    return jnp.dot(left, right, preferred_element_type=jnp.float32)


def by_owner(tokens, base_weight, adapter_a, adapter_b, cotangent, adapter_ids):
    owners = lax.axis_size("adapter")
    cores = lax.axis_size("mp")
    token_count, width = tokens.shape
    slot_rows = 4 * token_count // (3 * owners)
    column_part = width // cores
    member = lax.axis_index("mp")
    owner_ids = jnp.arange(owners, dtype=jnp.int32)
    onehot = (adapter_ids[:, None] == owner_ids[None, :]).astype(jnp.int32)
    ranking = jnp.sum((jnp.cumsum(onehot, axis=0) - 1) * onehot, axis=1)
    target = adapter_ids * slot_rows + ranking

    def exchange(rows):
        there = lax.all_to_all(
            rows.reshape(owners, slot_rows, rows.shape[1]),
            "adapter",
            split_axis=0,
            concat_axis=0,
            tiled=True,
        )
        return there.reshape(owners * slot_rows, rows.shape[1])

    def slotted(rows):
        return jnp.zeros((owners * slot_rows, rows.shape[1]), rows.dtype).at[target].set(rows)

    arrived = exchange(slotted(tokens))
    incoming_gradient = exchange(slotted(cotangent))
    own_a = adapter_a[0]
    own_b = adapter_b[0]
    feature_cols = lax.dynamic_slice_in_dim(arrived, member * column_part, column_part, 1)
    low = contract_cols(arrived, own_a).astype(jnp.bfloat16)
    value_update = (adapter_scale * matmul(low, own_b)).astype(jnp.bfloat16)
    delta_tokens = exchange(value_update)[target]
    base = matmul(tokens, lax.all_gather(base_weight, "dp", axis=0, tiled=True))
    projected = (base + delta_tokens.astype(jnp.float32)).astype(jnp.bfloat16)
    backward_total = lax.psum(contract_cols(incoming_gradient, own_b), "mp")
    backward_rows = (adapter_scale * backward_total).astype(jnp.bfloat16)
    up_term = adapter_scale * reduce_over_rows(low, incoming_gradient)
    term_a = reduce_over_rows(backward_rows, feature_cols)
    return (
        projected,
        lax.psum_scatter(term_a[None], "dp", scatter_dimension=1, tiled=True),
        lax.psum_scatter(up_term[None], "dp", scatter_dimension=1, tiled=True),
    )


AXES = ("dp", "adapter", "mp")
HBM = pl.BlockSpec(memory_space=pl.ANY)
VMEM = pl.BlockSpec(memory_space=pltpu.VMEM)


def like(shape, dtype):
    return jax.ShapeDtypeStruct(shape, dtype)


def call(kernel, outs, args, scratch=(), held=(), kept=None):
    return pl.pallas_call(
        kernel,
        out_shape=outs,
        in_specs=[VMEM if k in held else HBM for k in range(len(args))],
        out_specs=[VMEM if kept is None or k in kept else HBM for k in range(len(outs))],
        scratch_shapes=scratch,
        compiler_params=pltpu.CompilerParams(vmem_limit_bytes=56 << 20),
        cost_estimate=pl.CostEstimate(flops=1000, bytes_accessed=1000, transcendentals=0),
    )(*args)


def column_blocks(core, side, owner, half, block):
    first = ((core * half * 2 + side) * 2 + owner) * block
    return [pl.multiple_of(first + 4 * j * block, block) for j in range(half)]


def through(moves, stages, sems):
    ins, outs = [], []
    for k, (source, target) in enumerate(moves):
        ins.append(pltpu.make_async_copy(source, stages[k], sems.at[0, k]))
        outs.append(pltpu.make_async_copy(stages[k], target, sems.at[1, k]))
    return ins, outs


def coordinates():
    return lax.axis_index("dp") % 2, lax.axis_index("adapter"), lax.axis_index("mp")


def pack_first(block, tokens, ids, own_b, cotangent, out_x, out_grads, stage, grads, sems, last):
    x, y, c = coordinates()
    count, part = out_x.shape
    half = part // block
    padded = count + 8
    moves = [
        (tokens.at[:, pl.ds(start, block)], out_x.at[:, pl.ds(j * block, block)])
        for j, start in enumerate(column_blocks(c, 1 - x, y, half, block))
    ]
    copies = [
        pltpu.make_async_copy(cotangent, grads.at[pl.ds(0, count)], last.at[0]),
        pltpu.make_async_copy(own_b, grads.at[pl.ds(padded, own_b.shape[0])], last.at[1]),
    ]
    ins, outs = through(moves, [stage.at[j] for j in range(half)], sems)
    for copy in copies + ins:
        copy.start()
    grads[count:padded, :count] = (
        jnp.broadcast_to(ids[...], (8, count)).astype(jnp.float32).astype(grads.dtype)
    )
    grads[count:padded, count:] = jnp.zeros((8, grads.shape[1] - count), grads.dtype)
    for copy in copies:
        copy.wait()
    send = pltpu.make_async_copy(grads, out_grads, last.at[2])
    send.start()
    for arrive, leave in zip(ins, outs):
        arrive.wait()
        leave.start()
    for copy in outs + [send]:
        copy.wait()


def pack_rest(
    block, tokens, own_a, out_y, out_d, out_here, out_other, down_here, down_other, stage, small, sems
):
    x, y, c = coordinates()
    count, part = out_d.shape
    rank = own_a.shape[0]
    half = part // block
    moves, stages = [], []
    for target, place in (
        (out_y, (c, x, 1 - y)),
        (out_d, (c, 1 - x, 1 - y)),
        (out_here, (c, x, y)),
        (out_other, (1 - c, x, y)),
    ):
        for j, start in enumerate(column_blocks(*place, half, block)):
            columns = pl.ds(j * block, block)
            stages.append(stage.at[len(stages)])
            moves.append((tokens.at[:, pl.ds(start, block)], target.at[pl.ds(0, count), columns]))
    used = 0
    for target, offset, place in (
        (out_y, count, (c, x, 1 - y)),
        (down_here, 0, (c, x, y)),
        (down_other, 0, (1 - c, x, y)),
    ):
        for j, start in enumerate(column_blocks(*place, half, block)):
            columns = pl.ds(j * block, block)
            stages.append(small.at[used])
            used += 1
            moves.append((own_a.at[:, pl.ds(start, block)], target.at[pl.ds(offset, rank), columns]))
    ins, outs = through(moves, stages, sems)
    for copy in ins:
        copy.start()
    for arrive, leave in zip(ins, outs):
        arrive.wait()
        leave.start()
    for copy in outs:
        copy.wait()


def source_terms(down_here, down_other, here, other, back, mask, grads):
    low = mask * (contract_cols(down_here, here) + contract_cols(down_other, other))
    high = low.astype(jnp.bfloat16)
    rest = (low - high.astype(jnp.float32)).astype(jnp.bfloat16)
    return matmul(back, here), matmul(high, grads), high, rest


def value_of(here, other, weight, part, high, rest, up):
    c = lax.axis_index("mp")
    return (
        matmul(here, weight[pl.ds(pl.multiple_of(c * part, part), part)])
        + matmul(other, weight[pl.ds(pl.multiple_of((1 - c) * part, part), part)])
        + reduce_over_rows(high, up)
        + reduce_over_rows(rest, up)
    )


def fetch(sources, targets, sems):
    copies = [
        pltpu.make_async_copy(source, target, sems.at[k])
        for k, (source, target) in enumerate(zip(sources, targets))
    ]
    for copy in copies:
        copy.start()
    return copies


def wait_all(copies):
    for copy in copies:
        copy.wait()


def early_kernel(count, *refs):
    ins, refs = refs[:14], refs[14:]
    total, highs, rests, up_map, back_d, mask_d, down_here, down_other = refs[:8]
    held, sems = refs[8:22], refs[22]
    waits = fetch(ins, held, sems)
    parts, others = held[6:12], held[:6] + held[12:]
    own, over_y, over_x, own2, over_y2, over_x2 = others[:6]
    part = parts[0].shape[1]
    rank = total.shape[0] // 2
    padded = count + 8
    wait_all(waits[:6])
    grads = [own[:padded], over_x[:padded], over_y[:padded], over_x[padded:]]
    grads2 = [own2[:padded], over_x2[:padded], over_y2[:padded], over_x2[padded:]]
    up_map[...] = jnp.concatenate([own[padded:], over_y[padded:]], axis=0)
    up = up_map[...]
    up2 = jnp.concatenate([own2[padded:], over_y2[padded:]], axis=0)
    mine = lax.broadcasted_iota(jnp.int32, (2 * rank, count), 0) < rank
    owner = lax.axis_index("adapter").astype(jnp.float32)
    backs, masks = [], []
    for s in range(4):
        ids = grads[s][count:].astype(jnp.float32)[:1, :count]
        same = jnp.where(ids == owner, adapter_scale, 0.0)
        mask = jnp.where(mine, same, adapter_scale - same)
        both = contract_cols(up, grads[s]) + contract_cols(up2, grads2[s])
        backs.append((mask * both[:, :count]).astype(jnp.bfloat16))
        masks.append(mask)
    back_d[...] = backs[3]
    mask_d[...] = masks[3]
    wait_all(waits[6:])
    here, other = parts[::2], parts[1::2]
    down_here[...] = jnp.concatenate([others[6][...], here[2][count:]], axis=0)
    down_other[...] = jnp.concatenate([others[7][...], other[2][count:]], axis=0)
    for s in range(3):
        grad, gained, highs[s], rests[s] = source_terms(
            down_here[...],
            down_other[...],
            here[s][:count],
            other[s][:count],
            backs[s],
            masks[s],
            grads[s][:count],
        )
        if s == 0:
            total[:, :part] = grad
            total[:, part:] = gained
        else:
            total[:, :part] += grad
            total[:, part:] += gained


def late_kernel(rows, *refs):
    ins, (terms, high, rest), held, (sums, sems) = refs[:8], refs[8:11], refs[11:19], refs[19:]
    grads, back, mask, down_here, down_other, here, other, total = held
    count, part = here.shape
    wait_all(
        fetch((ins[0].at[pl.ds(grads.shape[0], grads.shape[0])],) + ins[1:], held, sems)
    )
    grad, up, high[...], rest[...] = source_terms(
        down_here[...], down_other[...], here[...], other[...], back[...], mask[...], grads[:count]
    )
    sums[:, :part] = total[:, :part] + grad
    sums[:, part:] = total[:, part:] + up
    rank = sums.shape[0] // 2
    first = lax.axis_index("adapter") == 0
    for m in range(rank // rows):
        mine, theirs = sums[m * rows : (m + 1) * rows], sums[rank + m * rows : rank + (m + 1) * rows]
        terms[2 * m * rows : 2 * (m + 1) * rows] = jnp.concatenate(
            [jnp.where(first, mine, theirs), jnp.where(first, theirs, mine)], axis=0
        ).astype(terms.dtype)


def values_kernel(count, *refs):
    ins, values, held, sems = refs[:14], refs[14:18], refs[18:32], refs[32]
    copies = fetch(ins, held, sems)
    weight, up, highs, rests, high_d, rest_d = held[:6]
    parts = held[6:]
    wait_all(copies[:6])
    for k, s in enumerate((3, 1, 2, 0)):
        wait_all(copies[6 + 2 * k : 8 + 2 * k])
        here, other = parts[2 * k], parts[1 + 2 * k]
        values[s][...] = value_of(
            here[:count],
            other[:count],
            weight,
            here.shape[1],
            high_d[...] if s == 3 else highs[s],
            rest_d[...] if s == 3 else rests[s],
            up[...],
        ).astype(values[s].dtype)


def by_width(tokens, base_weight, adapter_a, adapter_b, cotangent, adapter_ids):
    members = lax.axis_size("dp")
    line = members // 2
    half = line // 2
    count, width = tokens.shape
    features = cotangent.shape[1]
    rank = adapter_a.shape[1]
    block = width // (4 * line)
    part = half * block
    rows = rank // members
    padded = count + 8
    bf16, f32 = jnp.bfloat16, jnp.float32
    y = lax.axis_index("adapter")

    def swap(array, dx=0, dy=0, dc=0):
        pairs = []
        for here in range(members * 4):
            at_z, at_x, at_y, at_c = here // 8, here // 4 % 2, here // 2 % 2, here % 2
            there = ((at_z * 2 + (at_x ^ dx)) * 2 + (at_y ^ dy)) * 2 + (at_c ^ dc)
            pairs.append((here, there))
        return lax.ppermute(array, AXES, pairs)

    own_a, own_b = adapter_a[0], adapter_b[0]
    send_x, grads_own = call(
        functools.partial(pack_first, block),
        (like((count, part), bf16), like((padded + rank, features), bf16)),
        (tokens, adapter_ids[None], own_b, cotangent),
        scratch=[
            pltpu.VMEM((half, count, block), bf16),
            pltpu.VMEM((padded + rank, features), bf16),
            pltpu.SemaphoreType.DMA((2, half)),
            pltpu.SemaphoreType.DMA((3,)),
        ],
        held=(1,),
        kept=(),
    )
    own_a, send_x = lax.optimization_barrier((own_a, send_x))
    send_y, send_d, here_own, other_own, down_here, down_other = call(
        functools.partial(pack_rest, block),
        (like((count + rank, part), bf16),)
        + (like((count, part), bf16),) * 3
        + (like((rank, part), bf16),) * 2,
        (tokens, own_a),
        scratch=[
            pltpu.VMEM((4 * half, count, block), bf16),
            pltpu.VMEM((3 * half, rank, block), bf16),
            pltpu.SemaphoreType.DMA((2, 7 * half)),
        ],
        kept=(),
    )
    grads_y = swap(grads_own, dy=1)
    grads_y, send_y = lax.optimization_barrier((grads_y, send_y))
    part_x, part_y = swap(send_x, dx=1), swap(send_y, dy=1)
    own_weight = lax.dynamic_slice_in_dim(base_weight, y * block, block, 0)
    part_x, send_d, grads_y = lax.optimization_barrier((part_x, send_d, grads_y))
    grads_x = swap(jnp.concatenate([grads_own[:padded], grads_y[:padded]], axis=0), dx=1)
    part_d = swap(send_d, dx=1, dy=1)
    part_x, part_y, grads_x = lax.optimization_barrier((part_x, part_y, grads_x))
    weight = lax.all_to_all(
        jnp.tile(own_weight, (line, 1)),
        "dp",
        split_axis=0,
        concat_axis=0,
        tiled=True,
        axis_index_groups=[[2 * k + side for k in range(line)] for side in range(2)],
    )
    grads = (grads_own, grads_y, grads_x)
    parts = (here_own, other_own, part_x, swap(part_x, dc=1), part_y, swap(part_y, dc=1))
    args = (*grads, *(swap(array, dc=1) for array in grads), *parts, down_here, down_other)
    total, highs, rests, up_map, back_d, mask_d, down_here, down_other = call(
        functools.partial(early_kernel, count),
        (
            like((2 * rank, part + features), f32),
            like((3, 2 * rank, count), bf16),
            like((3, 2 * rank, count), bf16),
            like((2 * rank, features), bf16),
            like((2 * rank, count), bf16),
            like((2 * rank, count), f32),
            like((2 * rank, part), bf16),
            like((2 * rank, part), bf16),
        ),
        args,
        scratch=[pltpu.VMEM(array.shape, array.dtype) for array in args]
        + [pltpu.SemaphoreType.DMA((len(args),))],
    )
    part_d, total = lax.optimization_barrier((part_d, total))
    parts_d = (part_d, swap(part_d, dc=1))
    args = (grads_x, back_d, mask_d, down_here, down_other, *parts_d, total)
    terms, high_d, rest_d = call(
        functools.partial(late_kernel, rows),
        (
            like((2 * rank, part + features), bf16),
            like((2 * rank, count), bf16),
            like((2 * rank, count), bf16),
        ),
        args,
        scratch=[pltpu.VMEM((padded, features), bf16)]
        + [pltpu.VMEM(array.shape, array.dtype) for array in args[1:]]
        + [pltpu.VMEM(total.shape, f32), pltpu.SemaphoreType.DMA((len(args),))],
    )
    gathered = lax.all_to_all(terms, ("dp", "adapter"), split_axis=0, concat_axis=0, tiled=True)
    args = (weight, up_map, highs, rests, high_d, rest_d, *parts_d, *parts[2:], *parts[:2])
    value, value_x, value_y, value_d = call(
        functools.partial(values_kernel, count),
        (like((count, features), f32),) + (like((count, features), bf16),) * 3,
        args,
        scratch=[pltpu.VMEM(array.shape, array.dtype) for array in args]
        + [pltpu.SemaphoreType.DMA((len(args),))],
    )
    value_x, value_y, value_d = swap(value_x, dx=1), swap(value_y, dy=1), swap(value_d, dx=1, dy=1)
    gathered = gathered.reshape(line, 2, 2, rows, part + features)
    sums = jnp.sum(gathered.astype(f32), axis=0)
    up_gradient = jnp.sum(sums[..., part:], axis=(0, 1))[None]
    grad_a = jnp.concatenate(
        [
            sums[side, owner, :, j * block : (j + 1) * block]
            for j in range(half)
            for side in range(2)
            for owner in range(2)
        ],
        axis=1,
    )[None]
    value_x, value_y, value_d, grad_a = lax.optimization_barrier((value_x, value_y, value_d, grad_a))
    partial = lax.optimization_barrier(value + value_x.astype(f32))
    projected = (partial + value_y.astype(f32) + value_d.astype(f32)).astype(bf16)
    return projected, grad_a, up_gradient


def solution(mesh):
    line = mesh.shape["dp"] // 2
    square = mesh.shape["adapter"] == 2 and mesh.shape["mp"] == 2 and mesh.shape["dp"] % 4 == 0
    return jax.shard_map(
        by_width if square and line & (line - 1) == 0 else by_owner,
        mesh=mesh,
        in_specs=(
            P(("dp", "adapter"), None),
            P("dp", "mp"),
            P("adapter", None, None),
            P("adapter", None, "mp"),
            P(("dp", "adapter"), "mp"),
            P(("dp", "adapter")),
        ),
        out_specs=(P(("dp", "adapter"), "mp"), P("adapter", "dp", "mp"), P("adapter", "dp", "mp")),
        check_vma=False,
    )
```
